32 devices in a mesh: plane: 4 (over y, core), frame: 8 (over z, x).
Axes of the slice: x: 2, y: 2, z: 4, core: 2. Of those that a mesh axis runs over, the one named last changes fastest.
Arguments:
- image: float32 [8, 8, 2, 128, 128], P('plane', 'frame'), may hold values from -6 to 6
- sens: bfloat16 [4, 8, 2, 128, 128], P(None, 'plane'), may hold values from -3 to 3
- kspace: bfloat16 [4, 8, 8, 2, 128, 128], P(None, 'plane', 'frame'), may hold values from -6 to 6
- offsets: int32 [8, 128], P('frame'), may hold values from 0 to 3
- shifts: int32 [2], replicated, may hold values from 0 to 7
- step_size: float32 [1], replicated, may hold values from 0.5 to 1.5
- threshold: float32 [1], replicated, may hold values from 100 to 1000
Outputs:
- new_image: float32 [8, 8, 2, 128, 128], P('plane', 'frame')
The draws below stay inside these ranges and needn't reach their ends.
All inputs are finite; a program needn't handle non-finite values.
Results may differ from the reference program's by a relative error of at most 0.0003.
Values sent between devices are 32-bit elements; how exact they have to be, the bound alone decides.
A program may use at most 64 MiB of HBM per device.

```python
import math
import jax
import jax.numpy as jnp
from jax import lax

NY = 128
NZ = 128
COILS = 4
PATCH_X = 4
PATCH_Y = 8
PATCH_Z = 8
ACCEL = 4
CENTER = 8
NX = 8
FRAMES = 8


def touch_ends(values, stream_key, low, top_value):
    dims = values.shape
    spot = [jax.random.randint(jax.random.fold_in(stream_key, axis), (), 0, dims[axis]) for axis in range(len(dims))]
    values = values.at[tuple(spot)].set(low)
    longest = dims.index(max(dims))
    spot[longest] = (spot[longest] + 1) % dims[longest]
    return values.at[tuple(spot)].set(top_value)


def block_scale(stream_key, extent, cuts, low, high):
    loudness, own = 1.0, jax.random.fold_in(stream_key, 6)
    for axis_at, blocks in cuts:
        draws = jnp.exp(jax.random.uniform(jax.random.fold_in(own, axis_at), (blocks,), jnp.float32, low / len(cuts), high / len(cuts)))
        loudness = loudness * jnp.repeat(draws, extent[axis_at] // blocks).reshape([-1 if axis == axis_at else 1 for axis in range(len(extent))])
    return loudness


def bell_draw(stream_key, shape, deviation, most, split=(), held_as=jnp.bfloat16):
    values = deviation * jax.random.normal(stream_key, shape, jnp.float32)
    if split:
        values = values * block_scale(stream_key, shape, split, -0.22, 0.18)
    return jnp.clip(values, -most, most).astype(held_as)


def setup_inputs(seed: int = 0) -> dict:
    key_list = jax.random.split(jax.random.key(seed), 8)
    return {
        "image": bell_draw(key_list[0], (NX, FRAMES, 2, NY, NZ), 1.0, 6.0, ((0, 4), (1, 8)), jnp.float32),
        "sens": bell_draw(key_list[1], (COILS, NX, 2, NY, NZ), 0.5, 3.0, ((1, 4),)),
        "kspace": bell_draw(key_list[2], (COILS, NX, FRAMES, 2, NY, NZ), 1.0, 6.0, ((1, 4), (2, 8))),
        "offsets": touch_ends(jax.random.randint(key_list[3], (FRAMES, NY), 0, ACCEL), jax.random.fold_in(key_list[3], 1), 0, ACCEL - 1).astype(jnp.int32),
        "shifts": jax.random.randint(key_list[4], (2,), 0, PATCH_Y).astype(jnp.int32),
        "step_size": jnp.clip(jax.random.uniform(key_list[5], (1,), jnp.float32, 0.5, 1.5), 0.5, 1.5),
        "threshold": jnp.clip(jnp.exp(jax.random.uniform(key_list[6], (1,), jnp.float32, math.log(100.0), math.log(1000.0))), 100.0, 1000.0),
    }


def rotate(casorati):
    frames2, voxels = (casorati.shape[-2], casorati.shape[-1])
    split_parts = casorati.reshape(casorati.shape[:-2] + (frames2 // 2, 2, voxels))
    turned = jnp.stack([-split_parts[..., 1, :], split_parts[..., 0, :]], axis=-2)
    return turned.reshape(casorati.shape)

def gram_of(casorati):
    twin = rotate(casorati)
    first = jnp.einsum('...av,...bv->...ab', casorati.astype(jnp.float32), casorati.astype(jnp.float32), precision=lax.Precision.HIGHEST, preferred_element_type=jnp.float32)
    second = jnp.einsum('...av,...bv->...ab', twin.astype(jnp.float32), twin.astype(jnp.float32), precision=lax.Precision.HIGHEST, preferred_element_type=jnp.float32)
    return first + second

def shrink(casorati, gram, level):
    order = gram.shape[-1]
    system = gram + level * jnp.eye(order, dtype=jnp.float32)
    factor = jnp.linalg.cholesky(system)
    forward_part = jax.scipy.linalg.solve_triangular(factor, casorati, lower=True)
    solved = jax.scipy.linalg.solve_triangular(factor, forward_part, lower=True, trans=1)
    return casorati - level * solved

def reference(image, sens, kspace, offsets, shifts, step_size, threshold):
    rows_y = jnp.arange(NY, dtype=jnp.int32)
    rows_z = jnp.arange(NZ, dtype=jnp.int32)
    low_y = (rows_y < CENTER) | (rows_y >= NY - CENTER)
    low_z = (rows_z < CENTER) | (rows_z >= NZ - CENTER)
    regular = (rows_z[None, None, :] + offsets[:, :, None]) % ACCEL == 0
    sampled = (regular | low_y[None, :, None] & low_z[None, None, :]).astype(jnp.float32)
    step = step_size[0]

    def plane_step(inputs):
        plane_img, plane_sens, plane_data = inputs
        xc = plane_img[:, 0] + 1j * plane_img[:, 1]
        coil_maps = plane_sens[:, 0].astype(jnp.float32) + 1j * plane_sens[:, 1].astype(jnp.float32)
        measured = plane_data[:, :, 0].astype(jnp.float32) + 1j * plane_data[:, :, 1].astype(jnp.float32)
        coil_images = coil_maps[:, None] * xc[None]
        spectra = jnp.fft.fft2(coil_images, norm='ortho')
        resid = sampled[None] * (spectra - measured)
        returned = jnp.fft.ifft2(resid, norm='ortho')
        grad = jnp.sum(jnp.conj(coil_maps)[:, None] * returned, axis=0)
        return plane_img - step * jnp.stack([grad.real, grad.imag], axis=1)
    moved = lax.map(plane_step, (image, jnp.moveaxis(sens, 1, 0), jnp.moveaxis(kspace, 1, 0)))
    rolled = jnp.roll(moved, (shifts[0], shifts[1]), axis=(3, 4))
    nxb, nyb, nzb = (NX // PATCH_X, NY // PATCH_Y, NZ // PATCH_Z)
    pieces = rolled.reshape(nxb, PATCH_X, FRAMES, 2, nyb, PATCH_Y, nzb, PATCH_Z)
    pieces = pieces.transpose(0, 4, 6, 2, 3, 1, 5, 7).reshape(nxb * nyb * nzb, 2 * FRAMES, PATCH_X * PATCH_Y * PATCH_Z)
    level = threshold[0]

    def one_patch(casorati):
        return shrink(casorati, gram_of(casorati), level)
    shrunk = lax.map(one_patch, pieces)
    placed = shrunk.reshape(nxb, nyb, nzb, FRAMES, 2, PATCH_X, PATCH_Y, PATCH_Z)
    placed = placed.transpose(0, 5, 3, 4, 1, 6, 2, 7).reshape(NX, FRAMES, 2, NY, NZ)
    return jnp.roll(placed, (-shifts[0], -shifts[1]), axis=(3, 4))
```

```python
import functools
import math

import jax
import jax.numpy as jnp
import numpy as np
from jax import lax
from jax.experimental import pallas as pl
from jax.experimental.pallas import tpu as pltpu
from jax.sharding import PartitionSpec as P

PATCH_X = 4
PATCH_Y = 8
PATCH_Z = 8
ACCEL = 4
CENTER = 8


def from_partner(block, axis, distance):
    count = lax.axis_size(axis)
    route = []
    for low in range(count):
        high = low | 1 << distance
        if high != low and high < count:
            route += [(low, high), (high, low)]
    return lax.ppermute(block, axis, route)


def dft_tables(length):
    indices = jnp.arange(length, dtype=jnp.int32)
    phases = indices[:, None] * indices[None, :] % length
    angles = phases.astype(jnp.float32) * (2.0 * math.pi / length)
    norm_scale = 1.0 / math.sqrt(length)
    return (jnp.cos(angles) * norm_scale, jnp.sin(angles) * norm_scale)


def along_z(stacked, right_table, sign, width_z):
    product = jnp.einsum(
        "...z,zw->...w",
        stacked,
        right_table,
        precision=lax.Precision.HIGHEST,
        preferred_element_type=jnp.float32,
    )
    cos_part = product[..., :width_z]
    sin_part = product[..., width_z:]
    real_part = cos_part[..., 0, :, :] + sign * sin_part[..., 1, :, :]
    imag_part = cos_part[..., 1, :, :] - sign * sin_part[..., 0, :, :]
    return jnp.stack([real_part, imag_part], axis=-3)


def along_y(stacked, left_table):
    shape_in = stacked.shape
    merged = stacked.reshape(shape_in[:-3] + (2 * shape_in[-2], shape_in[-1]))
    result = jnp.einsum(
        "ur,...rz->...uz",
        left_table,
        merged,
        precision=lax.Precision.HIGHEST,
        preferred_element_type=jnp.float32,
    )
    return result.reshape(shape_in)


def rotate(casorati):
    frames2, voxels = (casorati.shape[-2], casorati.shape[-1])
    split_parts = casorati.reshape(casorati.shape[:-2] + (frames2 // 2, 2, voxels))
    turned = jnp.stack([-split_parts[..., 1, :], split_parts[..., 0, :]], axis=-2)
    return turned.reshape(casorati.shape)


def gram_of(casorati):
    twin = rotate(casorati)
    first = jnp.einsum(
        "kav,kbv->kab",
        casorati,
        casorati,
        precision=lax.Precision.HIGHEST,
        preferred_element_type=jnp.float32,
    )
    second = jnp.einsum(
        "kav,kbv->kab",
        twin,
        twin,
        precision=lax.Precision.HIGHEST,
        preferred_element_type=jnp.float32,
    )
    return first + second


def shrink(casorati, gram, level):
    order = gram.shape[-1]
    system = gram + level * jnp.eye(order, dtype=jnp.float32)
    factor = jnp.linalg.cholesky(system)
    forward_part = jax.scipy.linalg.solve_triangular(factor, casorati, lower=True)
    solved = jax.scipy.linalg.solve_triangular(factor, forward_part, lower=True, trans=1)
    return casorati - level * solved


def local_general(image, sens, kspace, offsets, shifts, step_size, threshold):
    planes, frames_dev, _, width_y, width_z = image.shape
    frames = frames_dev * lax.axis_size("frame")
    cos_y, sin_y = dft_tables(width_y)
    cos_z, sin_z = dft_tables(width_z)
    right_table = jnp.concatenate([cos_z, sin_z], axis=1)
    left_forward = jnp.concatenate(
        [jnp.concatenate([cos_y, sin_y], axis=1), jnp.concatenate([-sin_y, cos_y], axis=1)], axis=0
    )
    left_inverse = jnp.concatenate(
        [jnp.concatenate([cos_y, -sin_y], axis=1), jnp.concatenate([sin_y, cos_y], axis=1)], axis=0
    )
    rows_y = jnp.arange(width_y, dtype=jnp.int32)
    rows_z = jnp.arange(width_z, dtype=jnp.int32)
    low_y = (rows_y < CENTER) | (rows_y >= width_y - CENTER)
    low_z = (rows_z < CENTER) | (rows_z >= width_z - CENTER)
    regular = (rows_z[None, None, :] + offsets[:, :, None]) % ACCEL == 0
    sampled = (regular | low_y[None, :, None] & low_z[None, None, :]).astype(jnp.float32)
    image_re = image[:, :, 0]
    image_im = image[:, :, 1]
    maps = sens.astype(jnp.float32)
    sens_re = maps[:, :, 0][:, :, None]
    sens_im = maps[:, :, 1][:, :, None]
    coil_re = sens_re * image_re[None] - sens_im * image_im[None]
    coil_im = sens_re * image_im[None] + sens_im * image_re[None]
    stacked = jnp.stack([coil_re, coil_im], axis=3)
    spectra = along_y(along_z(stacked, right_table, 1.0, width_z), left_forward)
    resid = sampled[None, None, :, None] * (spectra - kspace.astype(jnp.float32))
    returned = along_z(along_y(resid, left_inverse), right_table, -1.0, width_z)
    back_re = returned[:, :, :, 0]
    back_im = returned[:, :, :, 1]
    grad_re = jnp.sum(sens_re * back_re + sens_im * back_im, axis=0)
    grad_im = jnp.sum(sens_re * back_im - sens_im * back_re, axis=0)
    moved = image - step_size[0] * jnp.stack([grad_re, grad_im], axis=2)
    rolled = jnp.roll(moved, (shifts[0], shifts[1]), axis=(3, 4))
    nyb = width_y // PATCH_Y
    nzb = width_z // PATCH_Z
    voxels = planes * PATCH_Y * PATCH_Z
    blocks = rolled.reshape(planes, frames_dev, 2, nyb, PATCH_Y, nzb, PATCH_Z)
    blocks = blocks.transpose(3, 5, 1, 2, 0, 4, 6).reshape(nyb * nzb, frames_dev, 2, voxels)
    regrouped = lax.all_to_all(blocks, "frame", split_axis=0, concat_axis=1, tiled=True)
    count = regrouped.shape[0]
    casorati = regrouped.reshape(count, 2 * frames, voxels)
    level = threshold[0]
    parity = lax.axis_index("plane") % 2
    halfway = count // 2
    first_part = casorati[:halfway]
    second_part = casorati[halfway:]
    kept_part = jnp.where(parity == 0, first_part, second_part)
    outgoing = jnp.where(parity == 0, second_part, first_part)
    incoming = from_partner(outgoing, "plane", 0)
    complete = jnp.concatenate([kept_part, incoming], axis=2)
    finished = shrink(complete, gram_of(complete), level)
    own_part = finished[:, :, :voxels]
    returned_part = from_partner(finished[:, :, voxels:], "plane", 0)
    shrunk = jnp.where(
        parity == 0,
        jnp.concatenate([own_part, returned_part], axis=0),
        jnp.concatenate([returned_part, own_part], axis=0),
    )
    restored = lax.all_to_all(
        shrunk.reshape(count, frames, 2, voxels), "frame", split_axis=1, concat_axis=0, tiled=True
    )
    placed = restored.reshape(nyb, nzb, frames_dev, 2, planes, PATCH_Y, PATCH_Z)
    placed = placed.transpose(4, 2, 3, 0, 5, 1, 6).reshape(planes, frames_dev, 2, width_y, width_z)
    return jnp.roll(placed, (-shifts[0], -shifts[1]), axis=(3, 4))


def block_tables(length):
    indices = np.arange(length)
    angles = (indices[:, None] * indices[None, :] % length) * (2.0 * np.pi / length)
    cos = np.cos(angles) / np.sqrt(length)
    sin = np.sin(angles) / np.sqrt(length)
    rotation = np.block([[cos, sin], [-sin, cos]])
    high = rotation.astype(jnp.bfloat16)
    low = (rotation - high.astype(np.float64)).astype(jnp.bfloat16)
    return np.stack([high, low, high.T, low.T])


def halves(values):
    high = values.astype(jnp.bfloat16)
    return high, (values - high.astype(jnp.float32)).astype(jnp.bfloat16)


def mul(left, right):
    return jnp.dot(left, right, preferred_element_type=jnp.float32)


def from_right(values, high, low):
    value_high, value_low = halves(values)
    return mul(value_high, high) + mul(value_high, low) + mul(value_low, high)


def from_left(high, low, values):
    value_high, value_low = halves(values)
    return mul(high, value_high) + mul(low, value_high) + mul(high, value_low)


def rows_to_lanes(values, coils, width):
    parts = [
        jnp.concatenate([values[c * width : (c + 1) * width, k * width : (k + 1) * width] for c in range(coils)], axis=1)
        for k in range(2)
    ]
    return jnp.concatenate(parts, axis=0)


def lanes_to_rows(values, coils, width):
    parts = [
        jnp.concatenate([values[k * width : (k + 1) * width, c * width : (c + 1) * width] for k in range(2)], axis=1)
        for c in range(coils)
    ]
    return jnp.concatenate(parts, axis=0)


def moved_plane(p, coils, width, image_ref, sens_ref, kspace_ref, table_ref, step, sampled):
    image_re = image_ref[p, 0, 0]
    image_im = image_ref[p, 0, 1]
    stacked = []
    for c in range(coils):
        sens_re = sens_ref[c, p, 0].astype(jnp.float32)
        sens_im = sens_ref[c, p, 1].astype(jnp.float32)
        stacked.append(
            jnp.concatenate(
                [sens_re * image_re - sens_im * image_im, sens_re * image_im + sens_im * image_re], axis=1
            )
        )
    along = from_right(jnp.concatenate(stacked, axis=0), table_ref[2], table_ref[3])
    spectra = from_left(table_ref[0], table_ref[1], rows_to_lanes(along, coils, width))
    data = jnp.concatenate(
        [
            jnp.concatenate([kspace_ref[c, p, 0, k].astype(jnp.float32) for c in range(coils)], axis=1)
            for k in range(2)
        ],
        axis=0,
    )
    weight = jnp.concatenate([jnp.concatenate([sampled] * coils, axis=1)] * 2, axis=0)
    resid = weight * (spectra - data)
    back = from_left(table_ref[2], table_ref[3], resid)
    returned = from_right(lanes_to_rows(back, coils, width), table_ref[0], table_ref[1])
    grad_re = jnp.zeros_like(image_re)
    grad_im = jnp.zeros_like(image_im)
    for c in range(coils):
        back_re = returned[c * width : (c + 1) * width, :width]
        back_im = returned[c * width : (c + 1) * width, width:]
        sens_re = sens_ref[c, p, 0].astype(jnp.float32)
        sens_im = sens_ref[c, p, 1].astype(jnp.float32)
        grad_re += sens_re * back_re + sens_im * back_im
        grad_im += sens_re * back_im - sens_im * back_re
    return image_re - step * grad_re, image_im - step * grad_im


def sweep(matrix, order):
    for k in range(order):
        pivot = 1.0 / matrix[k, k][0]
        column = {}
        for i in range(order):
            if i > k:
                column[i] = matrix[i, k]
            elif i < k:
                column[i] = (matrix[k, i][0], -matrix[k, i][1])
        scaled = {i: (re * pivot, im * pivot) for i, (re, im) in column.items()}
        for i in column:
            for j in column:
                if j > i:
                    continue
                a_re, a_im = scaled[i]
                b_re, b_im = column[j]
                re, im = matrix[i, j]
                re = re - (a_re * b_re + a_im * b_im)
                if i != j:
                    im = im - (a_im * b_re - a_re * b_im)
                matrix[i, j] = (re, im)
        for i in column:
            if i > k:
                matrix[i, k] = scaled[i]
            else:
                matrix[k, i] = (scaled[i][0], -scaled[i][1])
        matrix[k, k] = (-pivot, None)
    return matrix


def step_kernel(
    planes, frames, group, coils, width_y, width_z,
    shifts_ref, step_ref, level_ref, offsets_ref, image_ref, sens_ref, kspace_ref, table_ref,
    out_ref,
    rolled, gathered, entries, inverse, finished, landed,
    send_out, recv_out, send_back, recv_back, own_out, own_back,
):
    total = frames * group
    plane_me = lax.axis_index("plane")
    frame_me = lax.axis_index("frame")
    part_me = lax.rem(plane_me, group)
    base = plane_me - part_me
    me = frame_me * group + part_me
    rows = PATCH_Y

    def device(index):
        return {"plane": base + lax.rem(index, group), "frame": index // group}

    barrier = pltpu.get_barrier_semaphore()
    for k in range(1, total):
        pl.semaphore_signal(barrier, inc=1, device_id=device(lax.rem(me + k, total)), device_id_type=pl.DeviceIdType.MESH)

    lane = lax.broadcasted_iota(jnp.int32, (width_y, width_z), 1)
    row = lax.broadcasted_iota(jnp.int32, (width_y, width_z), 0)
    offset = jnp.broadcast_to(offsets_ref[...].astype(jnp.float32), (width_z, width_y)).T
    wanted = jnp.where(offset == 0.0, 0.0, ACCEL - offset)
    regular = lax.rem(lane, ACCEL).astype(jnp.float32) == wanted
    low_y = (row < CENTER) | (row >= width_y - CENTER)
    low_z = (lane < CENTER) | (lane >= width_z - CENTER)
    sampled = (regular | (low_y & low_z)).astype(jnp.float32)

    sends = []
    for p in range(planes):
        moved = moved_plane(p, coils, width_y, image_ref, sens_ref, kspace_ref, table_ref, step_ref[0], sampled)
        for k in range(2):
            rolled[p, k] = pltpu.roll(pltpu.roll(moved[k], shifts_ref[0], 0), shifts_ref[1], 1)
        if p == 0:
            pl.semaphore_wait(barrier, total - 1)
        group_sends = []
        for k in range(1, total):
            target = lax.rem(me + k, total)
            copy = pltpu.make_async_remote_copy(
                src_ref=rolled.at[p, :, pl.ds(pl.multiple_of(target * rows, rows), rows), :],
                dst_ref=gathered.at[p, part_me, frame_me],
                send_sem=send_out.at[p, k],
                recv_sem=recv_out.at[p, k],
                device_id=device(target),
                device_id_type=pl.DeviceIdType.MESH,
            )
            copy.start()
            group_sends.append(copy)
        own = pltpu.make_async_copy(
            rolled.at[p, :, pl.ds(pl.multiple_of(me * rows, rows), rows), :],
            gathered.at[p, part_me, frame_me],
            own_out.at[p],
        )
        own.start()
        sends.append((group_sends, own))

    pairs = [(f, g) for f in range(frames) for g in range(f + 1)]
    for p in range(planes):
        group_sends, own = sends[p]
        own.wait()
        for copy in group_sends:
            copy.wait_recv()
        for n, (f, g) in enumerate(pairs):
            sum_re = None
            sum_im = None
            for q in range(group):
                f_re, f_im = gathered[p, q, f, 0], gathered[p, q, f, 1]
                g_re, g_im = gathered[p, q, g, 0], gathered[p, q, g, 1]
                re = f_re * g_re + f_im * g_im
                sum_re = re if sum_re is None else sum_re + re
                if f != g:
                    im = f_im * g_re - f_re * g_im
                    sum_im = im if sum_im is None else sum_im + im
            spot = f * frames + g
            entries[spot] = sum_re if p == 0 else entries[spot] + sum_re
            if f != g:
                spot = g * frames + f
                entries[spot] = sum_im if p == 0 else entries[spot] + sum_im

    one_row = lax.broadcasted_iota(jnp.int32, (width_z, width_z), 0) // PATCH_Z
    one_lane = lax.broadcasted_iota(jnp.int32, (width_z, width_z), 1) // PATCH_Z
    same = (one_row == one_lane).astype(jnp.bfloat16)
    cells = entries[...]
    shift = rows // 2
    while shift:
        cells = cells + pltpu.roll(cells, shift, 1)
        shift //= 2
    high, low = halves(cells.reshape(frames * frames * rows, width_z))
    entries[...] = (mul(high, same) + mul(low, same)).reshape(frames * frames, rows, width_z)

    level = level_ref[0]
    matrix = {}
    for f, g in pairs:
        if f == g:
            matrix[f, f] = (entries[f * frames + f] + level, None)
        else:
            matrix[f, g] = (entries[f * frames + g], entries[g * frames + f])
    matrix = sweep(matrix, frames)
    for f, g in pairs:
        inverse[f * frames + g] = matrix[f, g][0] * level
        if f != g:
            inverse[g * frames + f] = matrix[f, g][1] * level

    backs = []
    for r in range(group):
        q = lax.rem(part_me + 1 + r, group)
        for p in range(planes):
            values = [(gathered[p, q, g, 0], gathered[p, q, g, 1]) for g in range(frames)]
            for f in range(frames):
                re, im = values[f]
                for g in range(frames):
                    g_re, g_im = values[g]
                    if f == g:
                        w_re = inverse[f * frames + f]
                        re = re + w_re * g_re
                        im = im + w_re * g_im
                        continue
                    if f > g:
                        w_re, w_im = inverse[f * frames + g], inverse[g * frames + f]
                        re = re + (w_re * g_re - w_im * g_im)
                        im = im + (w_re * g_im + w_im * g_re)
                    else:
                        w_re, w_im = inverse[g * frames + f], inverse[f * frames + g]
                        re = re + (w_re * g_re + w_im * g_im)
                        im = im + (w_re * g_im - w_im * g_re)
                finished[q, f, p, 0] = re
                finished[q, f, p, 1] = im
        for k in range(frames):
            f = lax.rem(frame_me + k, frames)
            source = finished.at[q, f]
            if r == group - 1 and k == 0:
                copy = pltpu.make_async_copy(
                    source, landed.at[:, :, pl.ds(pl.multiple_of(me * rows, rows), rows), :], own_back
                )
                copy.start()
                backs.append((copy, True))
                continue
            copy = pltpu.make_async_remote_copy(
                src_ref=source,
                dst_ref=landed.at[:, :, pl.ds(pl.multiple_of(me * rows, rows), rows), :],
                send_sem=send_back.at[r, k],
                recv_sem=recv_back.at[r, k],
                device_id={"plane": base + q, "frame": f},
                device_id_type=pl.DeviceIdType.MESH,
            )
            copy.start()
            backs.append((copy, False))
    for copy, local in backs:
        if local:
            copy.wait()
        else:
            copy.wait_recv()
    for p in range(planes):
        for k in range(2):
            shift_y = lax.rem(width_y - shifts_ref[0], width_y)
            shift_z = lax.rem(width_z - shifts_ref[1], width_z)
            out_ref[p, 0, k] = pltpu.roll(pltpu.roll(landed[p, k], shift_y, 0), shift_z, 1)
    for group_sends, own in sends:
        for copy in group_sends:
            copy.wait_send()
    for copy, local in backs:
        if not local:
            copy.wait_send()


def local_fused(image, sens, kspace, offsets, shifts, step_size, threshold):
    planes, _, _, width_y, width_z = image.shape
    coils = sens.shape[0]
    frames = lax.axis_size("frame")
    group = PATCH_X // planes
    total = frames * group
    table = jnp.asarray(block_tables(width_y))
    vmem = pl.BlockSpec(memory_space=pltpu.VMEM)
    smem = pl.BlockSpec(memory_space=pltpu.SMEM)
    slab = (PATCH_Y, width_z)
    dma = pltpu.SemaphoreType.DMA
    return pl.pallas_call(
        functools.partial(step_kernel, planes, frames, group, coils, width_y, width_z),
        out_shape=jax.ShapeDtypeStruct(image.shape, jnp.float32),
        in_specs=[smem, smem, smem, vmem, vmem, vmem, vmem, vmem],
        out_specs=vmem,
        scratch_shapes=[
            pltpu.VMEM((planes, 2, width_y, width_z), jnp.float32),
            pltpu.VMEM((planes, group, frames, 2) + slab, jnp.float32),
            pltpu.VMEM((frames * frames,) + slab, jnp.float32),
            pltpu.VMEM((frames * frames,) + slab, jnp.float32),
            pltpu.VMEM((group, frames, planes, 2) + slab, jnp.float32),
            pltpu.VMEM((planes, 2, width_y, width_z), jnp.float32),
            dma((planes, total)),
            dma((planes, total)),
            dma((group, frames)),
            dma((group, frames)),
            dma((planes,)),
            dma(()),
        ],
        compiler_params=pltpu.CompilerParams(collective_id=0, has_side_effects=True),
        name="prox_step",
    )(shifts, step_size, threshold, offsets, image, sens, kspace, table)


def local(image, sens, kspace, offsets, shifts, step_size, threshold):
    planes, frames_dev, _, width_y, width_z = image.shape
    frames = frames_dev * lax.axis_size("frame")
    group = PATCH_X // planes
    one_block = frames * group * PATCH_Y == width_y and frames_dev == 1
    split = group > 1 and lax.axis_size("plane") % group == 0
    if one_block and split and width_y == width_z and width_z % 128 == 0:
        return local_fused(image, sens, kspace, offsets, shifts, step_size, threshold)
    return local_general(image, sens, kspace, offsets, shifts, step_size, threshold)


def solution(mesh):
    in_specs = (
        P("plane", "frame", None, None, None),
        P(None, "plane", None, None, None),
        P(None, "plane", "frame", None, None, None),
        P("frame", None),
        P(),
        P(),
        P(),
    )
    out_specs = P("plane", "frame", None, None, None)
    return jax.shard_map(local, mesh=mesh, in_specs=in_specs, out_specs=out_specs, check_vma=False)
```

```python
import functools
import math

import jax
import jax.numpy as jnp
import numpy as np
from jax import lax
from jax.experimental import pallas as pl
from jax.experimental.pallas import tpu as pltpu
from jax.sharding import PartitionSpec as P

PATCH_X = 4
PATCH_Y = 8
PATCH_Z = 8
ACCEL = 4
CENTER = 8


def from_partner(block, axis, distance):
    count = lax.axis_size(axis)
    route = []
    for low in range(count):
        high = low | 1 << distance
        if high != low and high < count:
            route += [(low, high), (high, low)]
    return lax.ppermute(block, axis, route)


def dft_tables(length):
    indices = jnp.arange(length, dtype=jnp.int32)
    phases = indices[:, None] * indices[None, :] % length
    angles = phases.astype(jnp.float32) * (2.0 * math.pi / length)
    norm_scale = 1.0 / math.sqrt(length)
    return (jnp.cos(angles) * norm_scale, jnp.sin(angles) * norm_scale)


def along_z(stacked, right_table, sign, width_z):
    product = jnp.einsum(
        "...z,zw->...w",
        stacked,
        right_table,
        precision=lax.Precision.HIGHEST,
        preferred_element_type=jnp.float32,
    )
    cos_part = product[..., :width_z]
    sin_part = product[..., width_z:]
    real_part = cos_part[..., 0, :, :] + sign * sin_part[..., 1, :, :]
    imag_part = cos_part[..., 1, :, :] - sign * sin_part[..., 0, :, :]
    return jnp.stack([real_part, imag_part], axis=-3)


def along_y(stacked, left_table):
    shape_in = stacked.shape
    merged = stacked.reshape(shape_in[:-3] + (2 * shape_in[-2], shape_in[-1]))
    result = jnp.einsum(
        "ur,...rz->...uz",
        left_table,
        merged,
        precision=lax.Precision.HIGHEST,
        preferred_element_type=jnp.float32,
    )
    return result.reshape(shape_in)


def rotate(casorati):
    frames2, voxels = (casorati.shape[-2], casorati.shape[-1])
    split_parts = casorati.reshape(casorati.shape[:-2] + (frames2 // 2, 2, voxels))
    turned = jnp.stack([-split_parts[..., 1, :], split_parts[..., 0, :]], axis=-2)
    return turned.reshape(casorati.shape)


def gram_of(casorati):
    twin = rotate(casorati)
    first = jnp.einsum(
        "kav,kbv->kab",
        casorati,
        casorati,
        precision=lax.Precision.HIGHEST,
        preferred_element_type=jnp.float32,
    )
    second = jnp.einsum(
        "kav,kbv->kab",
        twin,
        twin,
        precision=lax.Precision.HIGHEST,
        preferred_element_type=jnp.float32,
    )
    return first + second


def shrink(casorati, gram, level):
    order = gram.shape[-1]
    system = gram + level * jnp.eye(order, dtype=jnp.float32)
    factor = jnp.linalg.cholesky(system)
    forward_part = jax.scipy.linalg.solve_triangular(factor, casorati, lower=True)
    solved = jax.scipy.linalg.solve_triangular(factor, forward_part, lower=True, trans=1)
    return casorati - level * solved


def local_general(image, sens, kspace, offsets, shifts, step_size, threshold):
    planes, frames_dev, _, width_y, width_z = image.shape
    frames = frames_dev * lax.axis_size("frame")
    cos_y, sin_y = dft_tables(width_y)
    cos_z, sin_z = dft_tables(width_z)
    right_table = jnp.concatenate([cos_z, sin_z], axis=1)
    left_forward = jnp.concatenate(
        [jnp.concatenate([cos_y, sin_y], axis=1), jnp.concatenate([-sin_y, cos_y], axis=1)], axis=0
    )
    left_inverse = jnp.concatenate(
        [jnp.concatenate([cos_y, -sin_y], axis=1), jnp.concatenate([sin_y, cos_y], axis=1)], axis=0
    )
    rows_y = jnp.arange(width_y, dtype=jnp.int32)
    rows_z = jnp.arange(width_z, dtype=jnp.int32)
    low_y = (rows_y < CENTER) | (rows_y >= width_y - CENTER)
    low_z = (rows_z < CENTER) | (rows_z >= width_z - CENTER)
    regular = (rows_z[None, None, :] + offsets[:, :, None]) % ACCEL == 0
    sampled = (regular | low_y[None, :, None] & low_z[None, None, :]).astype(jnp.float32)
    image_re = image[:, :, 0]
    image_im = image[:, :, 1]
    maps = sens.astype(jnp.float32)
    sens_re = maps[:, :, 0][:, :, None]
    sens_im = maps[:, :, 1][:, :, None]
    coil_re = sens_re * image_re[None] - sens_im * image_im[None]
    coil_im = sens_re * image_im[None] + sens_im * image_re[None]
    stacked = jnp.stack([coil_re, coil_im], axis=3)
    spectra = along_y(along_z(stacked, right_table, 1.0, width_z), left_forward)
    resid = sampled[None, None, :, None] * (spectra - kspace.astype(jnp.float32))
    returned = along_z(along_y(resid, left_inverse), right_table, -1.0, width_z)
    back_re = returned[:, :, :, 0]
    back_im = returned[:, :, :, 1]
    grad_re = jnp.sum(sens_re * back_re + sens_im * back_im, axis=0)
    grad_im = jnp.sum(sens_re * back_im - sens_im * back_re, axis=0)
    moved = image - step_size[0] * jnp.stack([grad_re, grad_im], axis=2)
    rolled = jnp.roll(moved, (shifts[0], shifts[1]), axis=(3, 4))
    nyb = width_y // PATCH_Y
    nzb = width_z // PATCH_Z
    voxels = planes * PATCH_Y * PATCH_Z
    blocks = rolled.reshape(planes, frames_dev, 2, nyb, PATCH_Y, nzb, PATCH_Z)
    blocks = blocks.transpose(3, 5, 1, 2, 0, 4, 6).reshape(nyb * nzb, frames_dev, 2, voxels)
    regrouped = lax.all_to_all(blocks, "frame", split_axis=0, concat_axis=1, tiled=True)
    count = regrouped.shape[0]
    casorati = regrouped.reshape(count, 2 * frames, voxels)
    level = threshold[0]
    parity = lax.axis_index("plane") % 2
    halfway = count // 2
    first_part = casorati[:halfway]
    second_part = casorati[halfway:]
    kept_part = jnp.where(parity == 0, first_part, second_part)
    outgoing = jnp.where(parity == 0, second_part, first_part)
    incoming = from_partner(outgoing, "plane", 0)
    complete = jnp.concatenate([kept_part, incoming], axis=2)
    finished = shrink(complete, gram_of(complete), level)
    own_part = finished[:, :, :voxels]
    returned_part = from_partner(finished[:, :, voxels:], "plane", 0)
    shrunk = jnp.where(
        parity == 0,
        jnp.concatenate([own_part, returned_part], axis=0),
        jnp.concatenate([returned_part, own_part], axis=0),
    )
    restored = lax.all_to_all(
        shrunk.reshape(count, frames, 2, voxels), "frame", split_axis=1, concat_axis=0, tiled=True
    )
    placed = restored.reshape(nyb, nzb, frames_dev, 2, planes, PATCH_Y, PATCH_Z)
    placed = placed.transpose(4, 2, 3, 0, 5, 1, 6).reshape(planes, frames_dev, 2, width_y, width_z)
    return jnp.roll(placed, (-shifts[0], -shifts[1]), axis=(3, 4))


VMEM_BYTES = 24 * 1024 * 1024


def block_tables(length):
    indices = np.arange(length)
    angles = (indices[:, None] * indices[None, :] % length) * (2.0 * np.pi / length)
    cos = np.cos(angles) / np.sqrt(length)
    sin = np.sin(angles) / np.sqrt(length)
    rotation = np.block([[cos, sin], [-sin, cos]])
    high = rotation.astype(jnp.bfloat16)
    low = (rotation - high.astype(np.float64)).astype(jnp.bfloat16)
    return np.stack([high, low, high.T, low.T])


def halves(values):
    high = values.astype(jnp.bfloat16)
    return high, (values - high.astype(jnp.float32)).astype(jnp.bfloat16)


def mul(left, right):
    return jnp.dot(left, right, preferred_element_type=jnp.float32)


def from_right(values, high, low):
    value_high, value_low = halves(values)
    return mul(value_high, high) + mul(value_high, low) + mul(value_low, high)


def from_left(high, low, values):
    value_high, value_low = halves(values)
    return mul(high, value_high) + mul(low, value_high) + mul(high, value_low)


def rows_to_lanes(values, coils, width):
    parts = [
        jnp.concatenate([values[c * width : (c + 1) * width, k * width : (k + 1) * width] for c in range(coils)], axis=1)
        for k in range(2)
    ]
    return jnp.concatenate(parts, axis=0)


def lanes_to_rows(values, coils, width):
    parts = [
        jnp.concatenate([values[k * width : (k + 1) * width, c * width : (c + 1) * width] for k in range(2)], axis=1)
        for c in range(coils)
    ]
    return jnp.concatenate(parts, axis=0)


def moved_plane(loads, p, coils, width, image_ref, sens_ref, kspace_ref, table_ref, step, sampled):
    loads["image", p].wait()
    loads["sens", p].wait()
    image_re = image_ref[p, 0, 0]
    image_im = image_ref[p, 0, 1]
    stacked = []
    for c in range(coils):
        sens_re = sens_ref[c, p, 0].astype(jnp.float32)
        sens_im = sens_ref[c, p, 1].astype(jnp.float32)
        stacked.append(
            jnp.concatenate(
                [sens_re * image_re - sens_im * image_im, sens_re * image_im + sens_im * image_re], axis=1
            )
        )
    if p == 0:
        loads["inverse"].wait()
    along = from_right(jnp.concatenate(stacked, axis=0), table_ref[2], table_ref[3])
    if p == 0:
        loads["forward"].wait()
    spectra = from_left(table_ref[0], table_ref[1], rows_to_lanes(along, coils, width))
    loads["kspace", p].wait()
    data = jnp.concatenate(
        [
            jnp.concatenate([kspace_ref[c, p, 0, k].astype(jnp.float32) for c in range(coils)], axis=1)
            for k in range(2)
        ],
        axis=0,
    )
    weight = jnp.concatenate([jnp.concatenate([sampled] * coils, axis=1)] * 2, axis=0)
    resid = weight * (spectra - data)
    back = from_left(table_ref[2], table_ref[3], resid)
    returned = from_right(lanes_to_rows(back, coils, width), table_ref[0], table_ref[1])
    grad_re = jnp.zeros_like(image_re)
    grad_im = jnp.zeros_like(image_im)
    for c in range(coils):
        back_re = returned[c * width : (c + 1) * width, :width]
        back_im = returned[c * width : (c + 1) * width, width:]
        sens_re = sens_ref[c, p, 0].astype(jnp.float32)
        sens_im = sens_ref[c, p, 1].astype(jnp.float32)
        grad_re += sens_re * back_re + sens_im * back_im
        grad_im += sens_re * back_im - sens_im * back_re
    return image_re - step * grad_re, image_im - step * grad_im


def sweep(matrix, order):
    for k in range(order):
        pivot = 1.0 / matrix[k, k][0]
        column = {}
        for i in range(order):
            if i > k:
                column[i] = matrix[i, k]
            elif i < k:
                column[i] = (matrix[k, i][0], -matrix[k, i][1])
        scaled = {i: (re * pivot, im * pivot) for i, (re, im) in column.items()}
        for i in column:
            for j in column:
                if j > i:
                    continue
                a_re, a_im = scaled[i]
                b_re, b_im = column[j]
                re, im = matrix[i, j]
                re = re - (a_re * b_re + a_im * b_im)
                if i != j:
                    im = im - (a_im * b_re - a_re * b_im)
                matrix[i, j] = (re, im)
        for i in column:
            if i > k:
                matrix[i, k] = scaled[i]
            else:
                matrix[k, i] = (scaled[i][0], -scaled[i][1])
        matrix[k, k] = (-pivot, None)
    return matrix


def step_kernel(
    planes, frames, group, coils, width_y, width_z,
    shifts_ref, step_ref, level_ref, offsets_ref, image_hbm, sens_hbm, kspace_hbm, table_hbm,
    landed,
    image_ref, sens_ref, kspace_ref, table_ref, load_sem,
    rolled, gathered, entries, inverse, finished,
    send_out, recv_out, send_back, recv_back, own_out, own_back,
):
    total = frames * group
    plane_me = lax.axis_index("plane")
    frame_me = lax.axis_index("frame")
    part_me = lax.rem(plane_me, group)
    base = plane_me - part_me
    me = frame_me * group + part_me
    rows = PATCH_Y

    def flip(index, mask, count):
        bit = 1
        while bit < count:
            if mask & bit:
                index = index + bit - 2 * bit * lax.rem(index // bit, 2)
            bit *= 2
        return index

    def device(index):
        return {"plane": base + lax.rem(index, group), "frame": index // group}

    loads = {}

    def load(name, source, target):
        loads[name] = pltpu.make_async_copy(source, target, load_sem.at[len(loads)])
        loads[name].start()

    for p in range(planes):
        load(("image", p), image_hbm.at[p], image_ref.at[p])
        load(("sens", p), sens_hbm.at[:, p], sens_ref.at[:, p])
        if p == 0:
            load("inverse", table_hbm.at[2:4], table_ref.at[2:4])
            load("forward", table_hbm.at[0:2], table_ref.at[0:2])
        load(("kspace", p), kspace_hbm.at[:, p], kspace_ref.at[:, p])

    barrier = pltpu.get_barrier_semaphore()
    for k in range(1, total):
        pl.semaphore_signal(barrier, inc=1, device_id=device(flip(me, k, total)), device_id_type=pl.DeviceIdType.MESH)

    lane = lax.broadcasted_iota(jnp.int32, (width_y, width_z), 1)
    row = lax.broadcasted_iota(jnp.int32, (width_y, width_z), 0)
    offset = jnp.broadcast_to(offsets_ref[...].astype(jnp.float32), (width_z, width_y)).T
    wanted = jnp.where(offset == 0.0, 0.0, ACCEL - offset)
    regular = lax.rem(lane, ACCEL).astype(jnp.float32) == wanted
    low_y = (row < CENTER) | (row >= width_y - CENTER)
    low_z = (lane < CENTER) | (lane >= width_z - CENTER)
    sampled = (regular | (low_y & low_z)).astype(jnp.float32)

    sends = []
    for p in range(planes):
        moved = moved_plane(loads, p, coils, width_y, image_ref, sens_ref, kspace_ref, table_ref, step_ref[0], sampled)
        for k in range(2):
            rolled[p, k] = pltpu.roll(pltpu.roll(moved[k], shifts_ref[0], 0), shifts_ref[1], 1)
        if p == 0:
            pl.semaphore_wait(barrier, total - 1)
        group_sends = []
        for k in reversed(range(1, total)):
            target = flip(me, k, total)
            copy = pltpu.make_async_remote_copy(
                src_ref=rolled.at[p, :, pl.ds(pl.multiple_of(target * rows, rows), rows), :],
                dst_ref=gathered.at[p, part_me, frame_me],
                send_sem=send_out.at[p, k],
                recv_sem=recv_out.at[p, k],
                device_id=device(target),
                device_id_type=pl.DeviceIdType.MESH,
            )
            copy.start()
            group_sends.append(copy)
        own = pltpu.make_async_copy(
            rolled.at[p, :, pl.ds(pl.multiple_of(me * rows, rows), rows), :],
            gathered.at[p, part_me, frame_me],
            own_out.at[p],
        )
        own.start()
        sends.append((group_sends, own))

    pairs = [(f, g) for f in range(frames) for g in range(f + 1)]
    for p in range(planes):
        group_sends, own = sends[p]
        own.wait()
        for copy in group_sends:
            copy.wait_recv()
        for n, (f, g) in enumerate(pairs):
            sum_re = None
            sum_im = None
            for q in range(group):
                f_re, f_im = gathered[p, q, f, 0], gathered[p, q, f, 1]
                g_re, g_im = gathered[p, q, g, 0], gathered[p, q, g, 1]
                re = f_re * g_re + f_im * g_im
                sum_re = re if sum_re is None else sum_re + re
                if f != g:
                    im = f_im * g_re - f_re * g_im
                    sum_im = im if sum_im is None else sum_im + im
            spot = f * frames + g
            entries[spot] = sum_re if p == 0 else entries[spot] + sum_re
            if f != g:
                spot = g * frames + f
                entries[spot] = sum_im if p == 0 else entries[spot] + sum_im

    one_row = lax.broadcasted_iota(jnp.int32, (width_z, width_z), 0) // PATCH_Z
    one_lane = lax.broadcasted_iota(jnp.int32, (width_z, width_z), 1) // PATCH_Z
    same = (one_row == one_lane).astype(jnp.bfloat16)
    cells = entries[...]
    shift = rows // 2
    while shift:
        cells = cells + pltpu.roll(cells, shift, 1)
        shift //= 2
    high, low = halves(cells.reshape(frames * frames * rows, width_z))
    entries[...] = (mul(high, same) + mul(low, same)).reshape(frames * frames, rows, width_z)

    level = level_ref[0]
    matrix = {}
    for f, g in pairs:
        if f == g:
            matrix[f, f] = (entries[f * frames + f] + level, None)
        else:
            matrix[f, g] = (entries[f * frames + g], entries[g * frames + f])
    matrix = sweep(matrix, frames)
    for f, g in pairs:
        re, im = matrix[f, g]
        inverse[f, g, 0] = re * level
        if f != g:
            inverse[f, g, 1] = im * level
            inverse[g, f, 0] = re * level
            inverse[g, f, 1] = -im * level
        else:
            inverse[f, f, 1] = jnp.zeros_like(re)

    backs = []
    spot = pl.ds(pl.multiple_of(me * rows, rows), rows)
    for k in reversed(range(frames)):
        f = flip(frame_me, k, frames)
        weights = [(inverse[f, g, 0], inverse[f, g, 1]) for g in range(frames)]
        for r in reversed(range(group)):
            q = flip(part_me, r, group)
            for p in range(planes):
                re = gathered[p, q, f, 0]
                im = gathered[p, q, f, 1]
                for g in range(frames):
                    g_re, g_im = gathered[p, q, g, 0], gathered[p, q, g, 1]
                    w_re, w_im = weights[g]
                    re = re + (w_re * g_re - w_im * g_im)
                    im = im + (w_re * g_im + w_im * g_re)
                finished[q, f, p, 0] = re
                finished[q, f, p, 1] = im
            if k == 0 and r == 0:
                copy = pltpu.make_async_copy(finished.at[q, f], landed.at[:, 0, :, spot, :], own_back)
            else:
                copy = pltpu.make_async_remote_copy(
                    src_ref=finished.at[q, f],
                    dst_ref=landed.at[:, 0, :, spot, :],
                    send_sem=send_back.at[r, k],
                    recv_sem=recv_back.at[r, k],
                    device_id={"plane": base + q, "frame": f},
                    device_id_type=pl.DeviceIdType.MESH,
                )
            copy.start()
            backs.append((copy, k == 0 and r == 0))
    for copy, local in backs:
        if local:
            copy.wait()
        else:
            copy.wait_recv()
    for group_sends, own in sends:
        for copy in group_sends:
            copy.wait_send()
    for copy, local in backs:
        if not local:
            copy.wait_send()


def unroll_kernel(planes, width_y, width_z, shifts_ref, landed_ref, out_ref):
    shift_y = lax.rem(width_y - shifts_ref[0], width_y)
    shift_z = lax.rem(width_z - shifts_ref[1], width_z)
    for p in range(planes):
        for k in range(2):
            out_ref[p, 0, k] = pltpu.roll(pltpu.roll(landed_ref[p, 0, k], shift_y, 0), shift_z, 1)


def local_fused(image, sens, kspace, offsets, shifts, step_size, threshold):
    planes, _, _, width_y, width_z = image.shape
    coils = sens.shape[0]
    frames = lax.axis_size("frame")
    group = PATCH_X // planes
    total = frames * group
    table = jnp.asarray(block_tables(width_y))
    vmem = pl.BlockSpec(memory_space=pltpu.VMEM)
    smem = pl.BlockSpec(memory_space=pltpu.SMEM)
    hbm = pl.BlockSpec(memory_space=pltpu.HBM)
    slab = (PATCH_Y, width_z)
    dma = pltpu.SemaphoreType.DMA
    image, sens, kspace, table = [pltpu.with_memory_space_constraint(x, pltpu.HBM) for x in (image, sens, kspace, table)]
    landed = pl.pallas_call(
        functools.partial(step_kernel, planes, frames, group, coils, width_y, width_z),
        out_shape=jax.ShapeDtypeStruct(image.shape, jnp.float32),
        in_specs=[smem, smem, smem, vmem, hbm, hbm, hbm, hbm],
        out_specs=pl.BlockSpec(memory_space=pl.ANY),
        scratch_shapes=[
            pltpu.VMEM(image.shape, image.dtype),
            pltpu.VMEM(sens.shape, sens.dtype),
            pltpu.VMEM(kspace.shape, kspace.dtype),
            pltpu.VMEM(table.shape, table.dtype),
            dma((3 * planes + 2,)),
            pltpu.VMEM((planes, 2, width_y, width_z), jnp.float32),
            pltpu.VMEM((planes, group, frames, 2) + slab, jnp.float32),
            pltpu.VMEM((frames * frames,) + slab, jnp.float32),
            pltpu.VMEM((frames, frames, 2) + slab, jnp.float32),
            pltpu.VMEM((group, frames, planes, 2) + slab, jnp.float32),
            dma((planes, total)),
            dma((planes, total)),
            dma((group, frames)),
            dma((group, frames)),
            dma((planes,)),
            dma(()),
        ],
        compiler_params=pltpu.CompilerParams(collective_id=0, has_side_effects=True, vmem_limit_bytes=VMEM_BYTES),
        name="prox_step",
    )(shifts, step_size, threshold, offsets, image, sens, kspace, table)
    return pl.pallas_call(
        functools.partial(unroll_kernel, planes, width_y, width_z),
        out_shape=jax.ShapeDtypeStruct(image.shape, jnp.float32),
        in_specs=[smem, vmem],
        out_specs=vmem,
        compiler_params=pltpu.CompilerParams(vmem_limit_bytes=VMEM_BYTES),
        name="shift_back",
    )(shifts, landed)


def local(image, sens, kspace, offsets, shifts, step_size, threshold):
    planes, frames_dev, _, width_y, width_z = image.shape
    frames = frames_dev * lax.axis_size("frame")
    group = PATCH_X // planes
    one_block = frames * group * PATCH_Y == width_y and frames_dev == 1 and frames & (frames - 1) == 0
    split = group > 1 and group & (group - 1) == 0 and lax.axis_size("plane") % group == 0
    if one_block and split and width_y == width_z and width_z % 128 == 0:
        return local_fused(image, sens, kspace, offsets, shifts, step_size, threshold)
    return local_general(image, sens, kspace, offsets, shifts, step_size, threshold)


def solution(mesh):
    in_specs = (
        P("plane", "frame", None, None, None),
        P(None, "plane", None, None, None),
        P(None, "plane", "frame", None, None, None),
        P("frame", None),
        P(),
        P(),
        P(),
    )
    out_specs = P("plane", "frame", None, None, None)
    return jax.shard_map(local, mesh=mesh, in_specs=in_specs, out_specs=out_specs, check_vma=False)
```

```python
import functools
import math

import jax
import jax.numpy as jnp
import numpy as np
from jax import lax
from jax.experimental import pallas as pl
from jax.experimental.pallas import tpu as pltpu
from jax.sharding import PartitionSpec as P

PATCH_X = 4
PATCH_Y = 8
PATCH_Z = 8
ACCEL = 4
CENTER = 8


def from_partner(block, axis, distance):
    count = lax.axis_size(axis)
    route = []
    for low in range(count):
        high = low | 1 << distance
        if high != low and high < count:
            route += [(low, high), (high, low)]
    return lax.ppermute(block, axis, route)


def dft_tables(length):
    indices = jnp.arange(length, dtype=jnp.int32)
    phases = indices[:, None] * indices[None, :] % length
    angles = phases.astype(jnp.float32) * (2.0 * math.pi / length)
    norm_scale = 1.0 / math.sqrt(length)
    return (jnp.cos(angles) * norm_scale, jnp.sin(angles) * norm_scale)


def along_z(stacked, right_table, sign, width_z):
    product = jnp.einsum(
        "...z,zw->...w",
        stacked,
        right_table,
        precision=lax.Precision.HIGHEST,
        preferred_element_type=jnp.float32,
    )
    cos_part = product[..., :width_z]
    sin_part = product[..., width_z:]
    real_part = cos_part[..., 0, :, :] + sign * sin_part[..., 1, :, :]
    imag_part = cos_part[..., 1, :, :] - sign * sin_part[..., 0, :, :]
    return jnp.stack([real_part, imag_part], axis=-3)


def along_y(stacked, left_table):
    shape_in = stacked.shape
    merged = stacked.reshape(shape_in[:-3] + (2 * shape_in[-2], shape_in[-1]))
    result = jnp.einsum(
        "ur,...rz->...uz",
        left_table,
        merged,
        precision=lax.Precision.HIGHEST,
        preferred_element_type=jnp.float32,
    )
    return result.reshape(shape_in)


def rotate(casorati):
    frames2, voxels = (casorati.shape[-2], casorati.shape[-1])
    split_parts = casorati.reshape(casorati.shape[:-2] + (frames2 // 2, 2, voxels))
    turned = jnp.stack([-split_parts[..., 1, :], split_parts[..., 0, :]], axis=-2)
    return turned.reshape(casorati.shape)


def gram_of(casorati):
    twin = rotate(casorati)
    first = jnp.einsum(
        "kav,kbv->kab",
        casorati,
        casorati,
        precision=lax.Precision.HIGHEST,
        preferred_element_type=jnp.float32,
    )
    second = jnp.einsum(
        "kav,kbv->kab",
        twin,
        twin,
        precision=lax.Precision.HIGHEST,
        preferred_element_type=jnp.float32,
    )
    return first + second


def shrink(casorati, gram, level):
    order = gram.shape[-1]
    system = gram + level * jnp.eye(order, dtype=jnp.float32)
    factor = jnp.linalg.cholesky(system)
    forward_part = jax.scipy.linalg.solve_triangular(factor, casorati, lower=True)
    solved = jax.scipy.linalg.solve_triangular(factor, forward_part, lower=True, trans=1)
    return casorati - level * solved


def local_general(image, sens, kspace, offsets, shifts, step_size, threshold):
    planes, frames_dev, _, width_y, width_z = image.shape
    frames = frames_dev * lax.axis_size("frame")
    cos_y, sin_y = dft_tables(width_y)
    cos_z, sin_z = dft_tables(width_z)
    right_table = jnp.concatenate([cos_z, sin_z], axis=1)
    left_forward = jnp.concatenate(
        [jnp.concatenate([cos_y, sin_y], axis=1), jnp.concatenate([-sin_y, cos_y], axis=1)], axis=0
    )
    left_inverse = jnp.concatenate(
        [jnp.concatenate([cos_y, -sin_y], axis=1), jnp.concatenate([sin_y, cos_y], axis=1)], axis=0
    )
    rows_y = jnp.arange(width_y, dtype=jnp.int32)
    rows_z = jnp.arange(width_z, dtype=jnp.int32)
    low_y = (rows_y < CENTER) | (rows_y >= width_y - CENTER)
    low_z = (rows_z < CENTER) | (rows_z >= width_z - CENTER)
    regular = (rows_z[None, None, :] + offsets[:, :, None]) % ACCEL == 0
    sampled = (regular | low_y[None, :, None] & low_z[None, None, :]).astype(jnp.float32)
    image_re = image[:, :, 0]
    image_im = image[:, :, 1]
    maps = sens.astype(jnp.float32)
    sens_re = maps[:, :, 0][:, :, None]
    sens_im = maps[:, :, 1][:, :, None]
    coil_re = sens_re * image_re[None] - sens_im * image_im[None]
    coil_im = sens_re * image_im[None] + sens_im * image_re[None]
    stacked = jnp.stack([coil_re, coil_im], axis=3)
    spectra = along_y(along_z(stacked, right_table, 1.0, width_z), left_forward)
    resid = sampled[None, None, :, None] * (spectra - kspace.astype(jnp.float32))
    returned = along_z(along_y(resid, left_inverse), right_table, -1.0, width_z)
    back_re = returned[:, :, :, 0]
    back_im = returned[:, :, :, 1]
    grad_re = jnp.sum(sens_re * back_re + sens_im * back_im, axis=0)
    grad_im = jnp.sum(sens_re * back_im - sens_im * back_re, axis=0)
    moved = image - step_size[0] * jnp.stack([grad_re, grad_im], axis=2)
    rolled = jnp.roll(moved, (shifts[0], shifts[1]), axis=(3, 4))
    nyb = width_y // PATCH_Y
    nzb = width_z // PATCH_Z
    voxels = planes * PATCH_Y * PATCH_Z
    blocks = rolled.reshape(planes, frames_dev, 2, nyb, PATCH_Y, nzb, PATCH_Z)
    blocks = blocks.transpose(3, 5, 1, 2, 0, 4, 6).reshape(nyb * nzb, frames_dev, 2, voxels)
    regrouped = lax.all_to_all(blocks, "frame", split_axis=0, concat_axis=1, tiled=True)
    count = regrouped.shape[0]
    casorati = regrouped.reshape(count, 2 * frames, voxels)
    level = threshold[0]
    parity = lax.axis_index("plane") % 2
    halfway = count // 2
    first_part = casorati[:halfway]
    second_part = casorati[halfway:]
    kept_part = jnp.where(parity == 0, first_part, second_part)
    outgoing = jnp.where(parity == 0, second_part, first_part)
    incoming = from_partner(outgoing, "plane", 0)
    complete = jnp.concatenate([kept_part, incoming], axis=2)
    finished = shrink(complete, gram_of(complete), level)
    own_part = finished[:, :, :voxels]
    returned_part = from_partner(finished[:, :, voxels:], "plane", 0)
    shrunk = jnp.where(
        parity == 0,
        jnp.concatenate([own_part, returned_part], axis=0),
        jnp.concatenate([returned_part, own_part], axis=0),
    )
    restored = lax.all_to_all(
        shrunk.reshape(count, frames, 2, voxels), "frame", split_axis=1, concat_axis=0, tiled=True
    )
    placed = restored.reshape(nyb, nzb, frames_dev, 2, planes, PATCH_Y, PATCH_Z)
    placed = placed.transpose(4, 2, 3, 0, 5, 1, 6).reshape(planes, frames_dev, 2, width_y, width_z)
    return jnp.roll(placed, (-shifts[0], -shifts[1]), axis=(3, 4))


VMEM_BYTES = 24 * 1024 * 1024


def block_tables(length):
    indices = np.arange(length)
    angles = (indices[:, None] * indices[None, :] % length) * (2.0 * np.pi / length)
    cos = np.cos(angles) / np.sqrt(length)
    sin = np.sin(angles) / np.sqrt(length)
    parts = []
    for table in (cos, sin):
        high = table.astype(jnp.bfloat16)
        parts += [high, (table - high.astype(np.float64)).astype(jnp.bfloat16)]
    return np.stack(parts)


def lay_tables(parts_ref, table_ref, width):
    low, top = pl.ds(0, width), pl.ds(width, width)
    for k in range(2):
        cos, sin = parts_ref[k], parts_ref[2 + k]
        for table, upper, lower in ((k, sin, -sin), (2 + k, -sin, sin)):
            table_ref[table, low, low] = cos
            table_ref[table, top, top] = cos
            table_ref[table, low, top] = upper
            table_ref[table, top, low] = lower


def halves(values):
    high = values.astype(jnp.bfloat16)
    return high, (values - high.astype(jnp.float32)).astype(jnp.bfloat16)


def mul(left, right):
    return jnp.dot(left, right, preferred_element_type=jnp.float32)


def from_right(values, high, low):
    value_high, value_low = halves(values)
    return mul(value_high, high) + mul(value_high, low) + mul(value_low, high)


def from_left(high, low, values):
    value_high, value_low = halves(values)
    return mul(high, value_high) + mul(low, value_high) + mul(high, value_low)


def rows_to_lanes(values, coils, width):
    parts = [
        jnp.concatenate([values[c * width : (c + 1) * width, k * width : (k + 1) * width] for c in range(coils)], axis=1)
        for k in range(2)
    ]
    return jnp.concatenate(parts, axis=0)


def lanes_to_rows(values, coils, width):
    parts = [
        jnp.concatenate([values[k * width : (k + 1) * width, c * width : (c + 1) * width] for k in range(2)], axis=1)
        for c in range(coils)
    ]
    return jnp.concatenate(parts, axis=0)


def moved_plane(loads, start_later, p, coils, width, image_ref, sens_ref, kspace_ref, table_ref, step, sampled):
    loads["image", p].wait()
    loads["sens", p].wait()
    image_re = image_ref[p, 0, 0]
    image_im = image_ref[p, 0, 1]
    stacked = []
    for c in range(coils):
        sens_re = sens_ref[c, p, 0].astype(jnp.float32)
        sens_im = sens_ref[c, p, 1].astype(jnp.float32)
        stacked.append(
            jnp.concatenate(
                [sens_re * image_re - sens_im * image_im, sens_re * image_im + sens_im * image_re], axis=1
            )
        )
    along = from_right(jnp.concatenate(stacked, axis=0), table_ref[2], table_ref[3])
    spectra = from_left(table_ref[0], table_ref[1], rows_to_lanes(along, coils, width))
    loads["kspace", p].wait()
    if p == 0:
        start_later()
    data = jnp.concatenate(
        [
            jnp.concatenate([kspace_ref[c, p, 0, k].astype(jnp.float32) for c in range(coils)], axis=1)
            for k in range(2)
        ],
        axis=0,
    )
    weight = jnp.concatenate([jnp.concatenate([sampled] * coils, axis=1)] * 2, axis=0)
    resid = weight * (spectra - data)
    back = from_left(table_ref[2], table_ref[3], resid)
    returned = from_right(lanes_to_rows(back, coils, width), table_ref[0], table_ref[1])
    grad_re = jnp.zeros_like(image_re)
    grad_im = jnp.zeros_like(image_im)
    for c in range(coils):
        back_re = returned[c * width : (c + 1) * width, :width]
        back_im = returned[c * width : (c + 1) * width, width:]
        sens_re = sens_ref[c, p, 0].astype(jnp.float32)
        sens_im = sens_ref[c, p, 1].astype(jnp.float32)
        grad_re += sens_re * back_re + sens_im * back_im
        grad_im += sens_re * back_im - sens_im * back_re
    return image_re - step * grad_re, image_im - step * grad_im


def sweep(matrix, order):
    for k in range(order):
        pivot = 1.0 / matrix[k, k][0]
        column = {}
        for i in range(order):
            if i > k:
                column[i] = matrix[i, k]
            elif i < k:
                column[i] = (matrix[k, i][0], -matrix[k, i][1])
        scaled = {i: (re * pivot, im * pivot) for i, (re, im) in column.items()}
        for i in column:
            for j in column:
                if j > i:
                    continue
                a_re, a_im = scaled[i]
                b_re, b_im = column[j]
                re, im = matrix[i, j]
                re = re - (a_re * b_re + a_im * b_im)
                if i != j:
                    im = im - (a_im * b_re - a_re * b_im)
                matrix[i, j] = (re, im)
        for i in column:
            if i > k:
                matrix[i, k] = scaled[i]
            else:
                matrix[k, i] = (scaled[i][0], -scaled[i][1])
        matrix[k, k] = (-pivot, None)
    return matrix


def step_kernel(
    planes, frames, group, coils, width_y, width_z,
    shifts_ref, step_ref, level_ref, offsets_ref, image_hbm, sens_hbm, kspace_hbm, table_hbm,
    landed,
    image_ref, sens_ref, kspace_ref, parts_ref, table_ref, load_sem,
    wrapped, rolled, gathered, entries, inverse, finished,
    send_out, recv_out, send_back, recv_back, own_out, own_back,
):
    total = frames * group
    plane_me = lax.axis_index("plane")
    frame_me = lax.axis_index("frame")
    part_me = lax.rem(plane_me, group)
    base = plane_me - part_me
    me = frame_me * group + part_me
    rows = PATCH_Y

    def flip(index, mask, count):
        bit = 1
        while bit < count:
            if mask & bit:
                index = index + bit - 2 * bit * lax.rem(index // bit, 2)
            bit *= 2
        return index

    def device(index):
        return {"plane": base + lax.rem(index, group), "frame": index // group}

    loads = {}

    def load(name, source, target):
        loads[name] = pltpu.make_async_copy(source, target, load_sem.at[len(loads)])
        loads[name].start()

    def load_plane(p):
        load(("image", p), image_hbm.at[p], image_ref.at[p])
        load(("sens", p), sens_hbm.at[:, p], sens_ref.at[:, p])
        load(("kspace", p), kspace_hbm.at[:, p], kspace_ref.at[:, p])

    def start_later():
        for p in range(1, planes):
            load_plane(p)

    load("table", table_hbm, parts_ref)
    load_plane(0)

    barrier = pltpu.get_barrier_semaphore()
    for k in range(1, total):
        pl.semaphore_signal(barrier, inc=1, device_id=device(flip(me, k, total)), device_id_type=pl.DeviceIdType.MESH)

    lane = lax.broadcasted_iota(jnp.int32, (width_y, width_z), 1)
    row = lax.broadcasted_iota(jnp.int32, (width_y, width_z), 0)
    offset = jnp.broadcast_to(offsets_ref[...].astype(jnp.float32), (width_z, width_y)).T
    wanted = jnp.where(offset == 0.0, 0.0, ACCEL - offset)
    regular = lax.rem(lane, ACCEL).astype(jnp.float32) == wanted
    low_y = (row < CENTER) | (row >= width_y - CENTER)
    low_z = (lane < CENTER) | (lane >= width_z - CENTER)
    sampled = (regular | (low_y & low_z)).astype(jnp.float32)

    sends = []
    loads["table"].wait()
    lay_tables(parts_ref, table_ref, width_y)
    for p in range(planes):
        moved = moved_plane(loads, start_later, p, coils, width_y, image_ref, sens_ref, kspace_ref, table_ref, step_ref[0], sampled)
        for k in range(2):
            part = pltpu.roll(moved[k], shifts_ref[1], 1)
            wrapped[p, k, pl.ds(0, rows), :] = part[width_y - rows :]
            wrapped[p, k, pl.ds(rows, width_y), :] = part
            rolled[p, k] = wrapped[p, k, pl.ds(rows - shifts_ref[0], width_y), :]
        if p == 0:
            pl.semaphore_wait(barrier, total - 1)
        group_sends = []
        for k in reversed(range(1, total)):
            target = flip(me, k, total)
            copy = pltpu.make_async_remote_copy(
                src_ref=rolled.at[p, :, pl.ds(pl.multiple_of(target * rows, rows), rows), :],
                dst_ref=gathered.at[p, part_me, frame_me],
                send_sem=send_out.at[p, k],
                recv_sem=recv_out.at[p, k],
                device_id=device(target),
                device_id_type=pl.DeviceIdType.MESH,
            )
            copy.start()
            group_sends.append(copy)
        own = pltpu.make_async_copy(
            rolled.at[p, :, pl.ds(pl.multiple_of(me * rows, rows), rows), :],
            gathered.at[p, part_me, frame_me],
            own_out.at[p],
        )
        own.start()
        sends.append((group_sends, own))

    pairs = [(f, g) for f in range(frames) for g in range(f + 1)]
    for p in range(planes):
        group_sends, own = sends[p]
        own.wait()
        for copy in group_sends:
            copy.wait_recv()
        for n, (f, g) in enumerate(pairs):
            sum_re = None
            sum_im = None
            for q in range(group):
                f_re, f_im = gathered[p, q, f, 0], gathered[p, q, f, 1]
                g_re, g_im = gathered[p, q, g, 0], gathered[p, q, g, 1]
                re = f_re * g_re + f_im * g_im
                sum_re = re if sum_re is None else sum_re + re
                if f != g:
                    im = f_im * g_re - f_re * g_im
                    sum_im = im if sum_im is None else sum_im + im
            spot = f * frames + g
            entries[spot] = sum_re if p == 0 else entries[spot] + sum_re
            if f != g:
                spot = g * frames + f
                entries[spot] = sum_im if p == 0 else entries[spot] + sum_im

    one_row = lax.broadcasted_iota(jnp.int32, (width_z, width_z), 0) // PATCH_Z
    one_lane = lax.broadcasted_iota(jnp.int32, (width_z, width_z), 1) // PATCH_Z
    same = (one_row == one_lane).astype(jnp.bfloat16)
    cells = entries[...]
    shift = rows // 2
    while shift:
        cells = cells + pltpu.roll(cells, shift, 1)
        shift //= 2
    high, low = halves(cells.reshape(frames * frames * rows, width_z))
    entries[...] = (mul(high, same) + mul(low, same)).reshape(frames * frames, rows, width_z)

    level = level_ref[0]
    matrix = {}
    for f, g in pairs:
        if f == g:
            matrix[f, f] = (entries[f * frames + f] + level, None)
        else:
            matrix[f, g] = (entries[f * frames + g], entries[g * frames + f])
    matrix = sweep(matrix, frames)
    for f, g in pairs:
        re, im = matrix[f, g]
        inverse[f, g, 0] = re * level
        if f != g:
            inverse[f, g, 1] = im * level
            inverse[g, f, 0] = re * level
            inverse[g, f, 1] = -im * level
        else:
            inverse[f, f, 1] = jnp.zeros_like(re)

    backs = []
    spot = pl.ds(pl.multiple_of(me * rows, rows), rows)
    for k in reversed(range(frames)):
        f = flip(frame_me, k, frames)
        weights = [(inverse[f, g, 0], inverse[f, g, 1]) for g in range(frames)]
        for r in reversed(range(group)):
            q = flip(part_me, r, group)
            for p in range(planes):
                re = gathered[p, q, f, 0]
                im = gathered[p, q, f, 1]
                for g in range(frames):
                    g_re, g_im = gathered[p, q, g, 0], gathered[p, q, g, 1]
                    w_re, w_im = weights[g]
                    re = re + (w_re * g_re - w_im * g_im)
                    im = im + (w_re * g_im + w_im * g_re)
                finished[q, f, p, 0] = re
                finished[q, f, p, 1] = im
            if k == 0 and r == 0:
                copy = pltpu.make_async_copy(finished.at[q, f], landed.at[:, 0, :, spot, :], own_back)
            else:
                copy = pltpu.make_async_remote_copy(
                    src_ref=finished.at[q, f],
                    dst_ref=landed.at[:, 0, :, spot, :],
                    send_sem=send_back.at[r, k],
                    recv_sem=recv_back.at[r, k],
                    device_id={"plane": base + q, "frame": f},
                    device_id_type=pl.DeviceIdType.MESH,
                )
            copy.start()
            backs.append((copy, k == 0 and r == 0))
    for copy, local in backs:
        if local:
            copy.wait()
        else:
            copy.wait_recv()
    for group_sends, own in sends:
        for copy in group_sends:
            copy.wait_send()
    for copy, local in backs:
        if not local:
            copy.wait_send()


def unroll_kernel(planes, width_y, width_z, shifts_ref, landed_ref, out_ref, wrapped):
    shift_z = lax.rem(width_z - shifts_ref[1], width_z)
    for p in range(planes):
        for k in range(2):
            part = pltpu.roll(landed_ref[p, 0, k], shift_z, 1)
            wrapped[p, k, pl.ds(0, width_y), :] = part
            wrapped[p, k, pl.ds(width_y, PATCH_Y), :] = part[:PATCH_Y]
            out_ref[p, 0, k] = wrapped[p, k, pl.ds(shifts_ref[0], width_y), :]


def local_fused(image, sens, kspace, offsets, shifts, step_size, threshold):
    planes, _, _, width_y, width_z = image.shape
    coils = sens.shape[0]
    frames = lax.axis_size("frame")
    group = PATCH_X // planes
    total = frames * group
    table = jnp.asarray(block_tables(width_y))
    vmem = pl.BlockSpec(memory_space=pltpu.VMEM)
    smem = pl.BlockSpec(memory_space=pltpu.SMEM)
    hbm = pl.BlockSpec(memory_space=pltpu.HBM)
    slab = (PATCH_Y, width_z)
    dma = pltpu.SemaphoreType.DMA
    image, sens, kspace, table = [pltpu.with_memory_space_constraint(x, pltpu.HBM) for x in (image, sens, kspace, table)]
    landed = pl.pallas_call(
        functools.partial(step_kernel, planes, frames, group, coils, width_y, width_z),
        out_shape=jax.ShapeDtypeStruct(image.shape, jnp.float32),
        in_specs=[smem, smem, smem, vmem, hbm, hbm, hbm, hbm],
        out_specs=pl.BlockSpec(memory_space=pl.ANY),
        scratch_shapes=[
            pltpu.VMEM(image.shape, image.dtype),
            pltpu.VMEM(sens.shape, sens.dtype),
            pltpu.VMEM(kspace.shape, kspace.dtype),
            pltpu.VMEM(table.shape, table.dtype),
            pltpu.VMEM((4, 2 * width_y, 2 * width_y), table.dtype),
            dma((3 * planes + 1,)),
            pltpu.VMEM((planes, 2, width_y + PATCH_Y, width_z), jnp.float32),
            pltpu.VMEM((planes, 2, width_y, width_z), jnp.float32),
            pltpu.VMEM((planes, group, frames, 2) + slab, jnp.float32),
            pltpu.VMEM((frames * frames,) + slab, jnp.float32),
            pltpu.VMEM((frames, frames, 2) + slab, jnp.float32),
            pltpu.VMEM((group, frames, planes, 2) + slab, jnp.float32),
            dma((planes, total)),
            dma((planes, total)),
            dma((group, frames)),
            dma((group, frames)),
            dma((planes,)),
            dma(()),
        ],
        compiler_params=pltpu.CompilerParams(collective_id=0, has_side_effects=True, vmem_limit_bytes=VMEM_BYTES),
        name="prox_step",
    )(shifts, step_size, threshold, offsets, image, sens, kspace, table)
    return pl.pallas_call(
        functools.partial(unroll_kernel, planes, width_y, width_z),
        out_shape=jax.ShapeDtypeStruct(image.shape, jnp.float32),
        in_specs=[smem, vmem],
        out_specs=vmem,
        scratch_shapes=[pltpu.VMEM((planes, 2, width_y + PATCH_Y, width_z), jnp.float32)],
        compiler_params=pltpu.CompilerParams(vmem_limit_bytes=VMEM_BYTES),
        name="shift_back",
    )(shifts, landed)


def local(image, sens, kspace, offsets, shifts, step_size, threshold):
    planes, frames_dev, _, width_y, width_z = image.shape
    frames = frames_dev * lax.axis_size("frame")
    group = PATCH_X // planes
    one_block = frames * group * PATCH_Y == width_y and frames_dev == 1 and frames & (frames - 1) == 0
    split = group > 1 and group & (group - 1) == 0 and lax.axis_size("plane") % group == 0
    if one_block and split and width_y == width_z and width_z % 128 == 0:
        return local_fused(image, sens, kspace, offsets, shifts, step_size, threshold)
    return local_general(image, sens, kspace, offsets, shifts, step_size, threshold)


def solution(mesh):
    in_specs = (
        P("plane", "frame", None, None, None),
        P(None, "plane", None, None, None),
        P(None, "plane", "frame", None, None, None),
        P("frame", None),
        P(),
        P(),
        P(),
    )
    out_specs = P("plane", "frame", None, None, None)
    return jax.shard_map(local, mesh=mesh, in_specs=in_specs, out_specs=out_specs, check_vma=False)
```
